256 devices in a mesh: row: 8 (over z), col: 32 (over x, y, core).
Axes of the slice: x: 4, y: 4, z: 8, core: 2. Of those that a mesh axis runs over, the one named last changes fastest.
Arguments:
- a_trail: float32 [16384, 16384], P('row', 'col'), may hold values from -60 to 60, as said below
- a_panel: float32 [16384, 256], P(('row', 'col')), may hold values from -6 to 6
- l_panel: float32 [16384, 256], P(('row', 'col')), may hold values from -0.5 to 0.5
- a_diag: float32 [256, 256], replicated, may hold values from -60 to 60, as said below
- l_inverse: float32 [256, 256], replicated, may hold values from -4 to 4, as said below
Outputs:
- trail_out: float32 [16384, 16384], P('row', 'col')
- panel_out: float32 [16384, 256], P(('row', 'col'))
The draws below stay inside these ranges and needn't reach their ends.
Inputs may be any that keep to these rules, and one draw needn't show every extreme that they name: `a_trail`: symmetric. `a_diag`: symmetric. `l_inverse`: lower triangular with a positive diagonal.
All inputs are finite; a program needn't handle non-finite values.
Results may differ from the reference program's by a relative error of at most 0.0003.
Values sent between devices are 32-bit elements; how exact they have to be, the bound alone decides.
No kernel may reach another device: no remote copies, remote signals or barrier semaphores. Data moves between devices by JAX's collectives and lax.ppermute only.
A program may use at most 64 MiB of HBM per device.

```python
import jax
import jax.numpy as jnp
from jax import lax

M = 16384
NB = 256
NS_STEPS = 8


def draw_a_trail(key, part):
    base = jax.random.normal(jax.random.fold_in(key, 11), (M, M), jnp.float32)
    sym = (base + base.T) * 0.7071067811865476
    return jnp.clip(sym, -60.0, 60.0)


def draw_a_diag(key, part):
    base = jax.random.normal(jax.random.fold_in(key, 21), (NB, NB), jnp.float32)
    sym = (base + base.T) * 0.7071067811865476
    return jnp.clip(sym, -60.0, 60.0)


def draw_l_inverse(key, part):
    lower = jnp.tril(jnp.ones((NB, NB), jnp.float32), -1)
    spread = 0.5 * jnp.clip(jax.random.normal(jax.random.fold_in(key, 31), (NB, NB), jnp.float32), -6.0, 6.0)
    diag_vals = jax.random.uniform(jax.random.fold_in(key, 32), (NB,), jnp.float32, 0.8, 1.2)
    off_part = spread * lower / jnp.sqrt(jnp.float32(NB))
    return off_part + jnp.diag(diag_vals)


def block_levels(rng, extent, split, least, high):
    level = 1.0
    for axis_at, shards_of in split:
        heights = jax.random.uniform(jax.random.fold_in(jax.random.fold_in(rng, 6), axis_at), (shards_of,), jnp.float32, least / len(split), high / len(split))
        level = level * jnp.repeat(jnp.exp(heights), extent[axis_at] // shards_of).reshape((-1,) + (1,) * (len(extent) - 1 - axis_at))
    return level


def gaussian(rng, extent, width, most, pieces=(), kind=jnp.bfloat16):
    factor_of = block_levels(rng, extent, pieces, -0.22, 0.18) if pieces else 1.0
    result = jax.random.normal(rng, extent, jnp.float32) * width * factor_of
    return jnp.minimum(jnp.maximum(result, -most), most).astype(kind)


def setup_inputs(seed: int = 0) -> dict:
    splits = jax.random.split(jax.random.key(seed), 6)
    a_trail = draw_a_trail(jax.random.fold_in(splits[5], 71), 0)
    a_panel = gaussian(splits[1], (M, NB), 1.0, 6.0, ((0, 256),), jnp.float32)
    l_panel = gaussian(splits[2], (M, NB), 0.0625, 0.5, ((0, 256),), jnp.float32)
    a_diag = draw_a_diag(jax.random.fold_in(splits[5], 71), 0)
    l_inverse = draw_l_inverse(jax.random.fold_in(splits[5], 71), 0)
    return dict(a_trail=a_trail, a_panel=a_panel, l_panel=l_panel, a_diag=a_diag, l_inverse=l_inverse)


def product(left, right):
    return jnp.dot(left.astype(jnp.float32), right.astype(jnp.float32), precision=lax.Precision.HIGHEST, preferred_element_type=jnp.float32)

def newton_inverse(matrix):
    identity = jnp.eye(matrix.shape[0], dtype=jnp.float32)
    approx = identity
    for repeat in range(NS_STEPS):
        approx = product(approx, 2.0 * identity - product(matrix, approx))
    return approx

def right_solve(factor, values):
    return lax.linalg.triangular_solve(factor, values, left_side=False, lower=True, transpose_a=True)

def reference(a_trail, a_panel, l_panel, a_diag, l_inverse):
    a11_new = product(product(l_inverse, a_diag), l_inverse.T)
    solved = product(a_panel, l_inverse.T)
    half_term = 0.5 * product(l_panel, a11_new)
    first_y = solved - half_term
    panel_out = first_y - half_term
    updated = a_trail - (product(first_y, l_panel.T) + product(l_panel, first_y.T))
    all_rows = jnp.arange(M, dtype=jnp.int32)
    keep_mask = (all_rows >= NB)[:, None]
    next_panel = jnp.where(keep_mask, updated[:, :NB], 0.0)
    picker = (all_rows[:, None] - NB == jnp.arange(NB, dtype=jnp.int32)[None, :]).astype(jnp.float32)
    gram = product(next_panel.T, next_panel)
    top_block = next_panel[NB:2 * NB]
    factor = jnp.linalg.cholesky(gram)
    q_rows = right_solve(factor, next_panel)
    q_top = right_solve(factor, top_block)
    identity = jnp.eye(NB, dtype=jnp.float32)
    g_inverse = newton_inverse(identity + q_top).T
    y_full = q_rows + picker
    x_mat = product(product(updated, y_full), g_inverse)
    m_core = product(g_inverse.T, product(y_full.T, x_mat))
    z_mat = x_mat - 0.5 * product(y_full, m_core)
    trail_out = updated - (product(z_mat, y_full.T) + product(y_full, z_mat.T))
    return (trail_out, panel_out)
```

```python
import functools

import jax
import jax.numpy as jnp
from jax import lax
from jax.experimental import pallas as pl
from jax.experimental.pallas import tpu as pltpu
from jax.sharding import PartitionSpec as P

NS_STEPS = 8
ROWS = 8
COLS = 32
BOTH = ("row", "col")


def product(left, right):
    return jnp.dot(left, right, precision=lax.Precision.HIGHEST, preferred_element_type=jnp.float32)


def product3(left, right):
    return jnp.dot(left, right, precision=lax.Precision.HIGH, preferred_element_type=jnp.float32)


def right_solve(factor, values):
    return lax.linalg.triangular_solve(
        factor, values, left_side=False, lower=True, transpose_a=True
    )


def newton_inverse_of_shifted(top):
    size = top.shape[0]
    residual = -top
    approx = jnp.eye(size, dtype=jnp.float32) + residual
    for step in range(1, NS_STEPS):
        residual = product(residual, residual)
        approx = approx + product(approx, residual)
    return approx


def place(pieces, offsets, out_rows):
    arrays = []
    where = []
    for array, start, size in pieces:
        for at, known in enumerate(arrays):
            if known is array:
                break
        else:
            at = len(arrays)
            arrays.append(array)
        where.append((at, start, size))
    width = arrays[0].shape[1]
    count = len(where)

    def body(offs, *refs):
        sources = refs[: len(arrays)]
        out = refs[len(arrays)]
        sems = refs[len(arrays) + 1]
        copies = []
        for index, (at, start, size) in enumerate(where):
            copy = pltpu.make_async_copy(
                sources[at].at[pl.ds(start, size)],
                out.at[pl.ds(pl.multiple_of(offs[index], 8), size)],
                sems.at[index],
            )
            copy.start()
            copies.append(copy)
        for copy in copies:
            copy.wait()

    return pl.pallas_call(
        body,
        out_shape=jax.ShapeDtypeStruct((out_rows, width), jnp.float32),
        in_specs=[pl.BlockSpec(memory_space=pltpu.SMEM)] + [pl.BlockSpec(memory_space=pl.ANY)] * len(arrays),
        out_specs=pl.BlockSpec(memory_space=pl.ANY),
        scratch_shapes=[pltpu.SemaphoreType.DMA((count,))],
    )(jnp.stack(offsets).astype(jnp.int32), *arrays)


def col_shift(first_axis, step):
    def target(col):
        x, y, core = col // 8, (col // 2) % 4, col % 2
        if (core == 0) == first_axis:
            x = (x + step) % 4
        else:
            y = (y + step) % 4
        return x * 8 + y * 2 + core

    return [(col, target(col)) for col in range(COLS)]


def gather_cols(block):
    rows = block.shape[0]
    move = functools.partial(lax.ppermute, axis_name="col")

    def ring(value, first_axis):
        return [
            value,
            move(value, perm=col_shift(first_axis, -1)),
            move(value, perm=col_shift(first_axis, 2)),
            move(value, perm=col_shift(first_axis, 1)),
        ]

    own = ring(jnp.concatenate(ring(block, True), 0), False)
    other = [move(value, perm=[(col, col ^ 1) for col in range(COLS)]) for value in own]
    col = lax.axis_index("col")
    x, y, core = col // 8, (col // 2) % 4, col % 2
    pieces, offsets = [], []
    for values, its_core in ((own, core), (other, 1 - core)):
        for second in range(4):
            for first in range(4):
                step_x = jnp.where(its_core == 0, first, second)
                step_y = jnp.where(its_core == 0, second, first)
                at = ((x + step_x) % 4) * 8 + ((y + step_y) % 4) * 2 + its_core
                pieces.append((values[second], first * rows, rows))
                offsets.append(at * rows)
    return place(pieces, offsets, COLS * rows)


def gather_rows(block):
    rows = block.shape[0]
    row = lax.axis_index("row")
    pieces, offsets = [(block, 0, rows)], [row * rows]
    for step in range(1, ROWS):
        got = lax.ppermute(block, "row", [(at, (at + step) % ROWS) for at in range(ROWS)])
        pieces.append((got, 0, rows))
        offsets.append(((row - step) % ROWS) * rows)
    return place(pieces, offsets, ROWS * rows)


def to_columns(block):
    return lax.ppermute(
        block, BOTH, [(at, (at % 8) * COLS + at // 8) for at in range(ROWS * COLS)]
    )


def sum_rows(block):
    total = block
    for step in range(1, ROWS):
        total = total + lax.ppermute(block, "row", [(at, (at + step) % ROWS) for at in range(ROWS)])
    return total


def from_first_row(block):
    row = lax.axis_index("row")
    total = jnp.where(row == 0, block, 0.0)
    for step in range(1, ROWS):
        total = total + lax.ppermute(block, "row", [(0, step)])
    return total


def scatter_sum_cols(block):
    parts = lax.all_to_all(block, "col", 0, 0, tiled=True)
    return jnp.sum(parts.reshape(COLS, block.shape[0] // COLS, block.shape[1]), axis=0)


def shards(a_trail, a_panel, l_panel, a_diag, l_inverse):
    row_dev, col_dev = a_trail.shape
    nb = a_diag.shape[0]
    part = col_dev // ROWS
    row = lax.axis_index("row")
    col = lax.axis_index("col")

    raw_rows = gather_cols(jnp.concatenate([a_panel, l_panel], 1))

    a11_new = product(product(l_inverse, a_diag), l_inverse.T)
    half_term = 0.5 * product(l_panel, a11_new)
    first_y = product(a_panel, l_inverse.T) - half_term
    panel_out = first_y - half_term
    mates = gather_rows(to_columns(jnp.concatenate([product(l_panel, l_inverse), panel_out], 1)))
    updated = a_trail - product3(raw_rows, mates.T)

    local = lax.iota(jnp.int32, col_dev)
    not_top = jnp.logical_or(col > 0, local >= nb)
    head = updated[: 2 * nb]
    panel_t = jnp.where(not_top[None, :], head[:nb], 0.0)

    corner = jnp.where(col == 0, head[nb:], 0.0)
    packed = from_first_row(
        scatter_sum_cols(jnp.concatenate([product(panel_t, panel_t.T), corner], 1))
    )
    packed = gather_cols(packed)
    gram, top_block, corner = packed[:, :nb], packed[:, nb : 2 * nb], packed[:, 2 * nb :]

    flipped = jnp.concatenate([panel_t, head[nb:]], 0).T
    shard = None
    for at in range(ROWS):
        got = lax.ppermute(
            flipped[at * part : (at + 1) * part],
            BOTH,
            [(c, (c // 4) * COLS + (c % 4) * 8 + at) for c in range(COLS)],
        )
        shard = got if shard is None else shard + got
    both_rows = gather_cols(shard)
    both_cols = gather_rows(to_columns(shard))
    panel_rows, second_rows = both_rows[:, :nb], both_rows[:, nb:]
    panel_cols, second_cols = both_cols[:, :nb], both_cols[:, nb:]

    partial = product3(updated.T, panel_rows)
    image = None
    for step in range(ROWS):
        at = (row + step) % ROWS
        got = lax.ppermute(
            lax.dynamic_slice_in_dim(partial, at * part, part, 0),
            BOTH,
            [
                (r * COLS + c, (c // 4) * COLS + (c % 4) * 8 + (r + step) % ROWS)
                for r in range(ROWS)
                for c in range(COLS)
            ],
        )
        image = got if image is None else image + got
    image_rows = gather_cols(image)
    image_cols = gather_rows(to_columns(image))

    weights = jnp.concatenate(
        [product3(panel_cols.T, partial), jnp.where(col == 0, partial[nb : 2 * nb], 0.0)], 1
    )
    weights = gather_cols(sum_rows(scatter_sum_cols(weights)))
    core, image_top = weights[:, :nb], weights[:, nb:]

    factor = jnp.linalg.cholesky(gram)
    solve = right_solve(factor, jnp.eye(nb, dtype=jnp.float32))
    g_inverse = newton_inverse_of_shifted(product(top_block, solve)).T
    image_top = product(image_top, solve)
    middle = product(product(solve.T, core), solve) + image_top + image_top.T + corner
    m_core = product(g_inverse.T, product(middle, g_inverse))
    solve_g = product(solve, g_inverse)

    def reflectors(panel, image, second, owner):
        size = panel.shape[0]
        picker = jnp.logical_and(
            lax.iota(jnp.int32, size)[:, None] - nb == lax.iota(jnp.int32, nb)[None, :], owner
        ).astype(jnp.float32)
        y_part = product3(panel, solve) + picker
        x_part = product3(image, solve_g) + product3(second, g_inverse)
        return y_part, x_part - 0.5 * product3(y_part, m_core)

    y_rows, z_rows = reflectors(panel_rows, image_rows, second_rows, row == 0)
    y_cols, z_cols = reflectors(panel_cols, image_cols, second_cols, col == 0)
    trail_out = updated - product3(
        jnp.concatenate([z_rows, y_rows], 1), jnp.concatenate([y_cols, z_cols], 1).T
    )
    return (trail_out, panel_out)


def solution(mesh):
    return jax.shard_map(
        shards,
        mesh=mesh,
        in_specs=(P("row", "col"), P(("row", "col"), None), P(("row", "col"), None), P(), P()),
        out_specs=(P("row", "col"), P(("row", "col"), None)),
        check_vma=False,
    )
```

```python
import jax
import jax.numpy as jnp
from jax import lax
from jax.sharding import PartitionSpec as P

NS_STEPS = 8
ROWS = 8
COLS = 32
BOTH = ("row", "col")


def product(left, right):
    return jnp.dot(left, right, precision=lax.Precision.HIGHEST, preferred_element_type=jnp.float32)


def product3(left, right):
    return jnp.dot(left, right, precision=lax.Precision.HIGH, preferred_element_type=jnp.float32)


def right_solve(factor, values):
    return lax.linalg.triangular_solve(
        factor, values, left_side=False, lower=True, transpose_a=True
    )


def newton_inverse_of_shifted(top):
    size = top.shape[0]
    residual = -top
    approx = jnp.eye(size, dtype=jnp.float32) + residual
    for step in range(1, NS_STEPS):
        residual = product(residual, residual)
        approx = approx + product(approx, residual)
    return approx


def share(block, axis, size):
    parts = lax.all_to_all(jnp.tile(block, (size, 1)), axis, 0, 0, tiled=True)
    return parts.reshape((size,) + block.shape)


def gather_small(block, axis, size):
    return share(block, axis, size).reshape(size * block.shape[0], block.shape[1])


def scatter_sum(block, axis, size):
    parts = lax.all_to_all(block, axis, 0, 0, tiled=True)
    return jnp.sum(parts.reshape(size, block.shape[0] // size, block.shape[1]), axis=0)


def to_columns(block):
    return lax.ppermute(
        block, BOTH, [(at, (at % 8) * COLS + at // 8) for at in range(ROWS * COLS)]
    )


def to_panel(block):
    return lax.ppermute(
        block, BOTH, [((at % 8) * COLS + at // 8, at) for at in range(ROWS * COLS)]
    )


def scatter_from_first_row(block):
    size = block.shape[0] // ROWS
    total = jnp.where(lax.axis_index("row") == 0, block[:size], 0.0)
    for at in range(1, ROWS):
        total = total + lax.ppermute(block[at * size : (at + 1) * size], "row", [(0, at)])
    return total


def shards(a_trail, a_panel, l_panel, a_diag, l_inverse):
    row_dev, col_dev = a_trail.shape
    nb = a_diag.shape[0]
    part = col_dev // ROWS
    row = lax.axis_index("row")
    col = lax.axis_index("col")

    raw_rows = lax.all_gather(jnp.concatenate([a_panel, l_panel], 1), "col", axis=0, tiled=True)

    a11_new = product(product(l_inverse, a_diag), l_inverse.T)
    half_term = 0.5 * product(l_panel, a11_new)
    first_y = product(a_panel, l_inverse.T) - half_term
    panel_out = first_y - half_term
    mates = gather_small(
        to_columns(jnp.concatenate([product(l_panel, l_inverse), panel_out], 1)), "row", ROWS
    )
    updated = a_trail - product3(raw_rows, mates.T)

    local = lax.iota(jnp.int32, col_dev)
    not_top = jnp.logical_or(col > 0, local >= nb)
    head = updated[: 2 * nb]
    panel_t = jnp.where(not_top[None, :], head[:nb], 0.0)

    shard = scatter_from_first_row(jnp.concatenate([panel_t, head[nb:]], 0).T)
    both_rows = lax.all_gather(to_panel(shard), "col", axis=0, tiled=True)
    panel_rows, second_rows = both_rows[:, :nb], both_rows[:, nb:]

    corner = jnp.where(col == 0, head[nb:], 0.0)
    packed = scatter_sum(
        jnp.concatenate([product(panel_t, panel_t.T), corner], 1), "col", COLS
    )
    packed = gather_small(share(packed, "row", ROWS)[0], "col", COLS)
    gram, top_block, corner = packed[:, :nb], packed[:, nb : 2 * nb], packed[:, 2 * nb :]

    partial = product3(updated.T, panel_rows)
    image = scatter_sum(partial, "row", ROWS)
    image_rows = lax.all_gather(to_panel(image), "col", axis=0, tiled=True)
    cols = lax.all_gather(jnp.concatenate([shard, image], 1), "row", axis=0, tiled=True)
    panel_cols, second_cols, image_cols = cols[:, :nb], cols[:, nb : 2 * nb], cols[:, 2 * nb :]

    weights = jnp.concatenate(
        [product(shard[:, :nb].T, image), jnp.where(col == 0, partial[nb : 2 * nb], 0.0)], 1
    )
    weights = scatter_sum(weights, "col", COLS)
    weights = gather_small(jnp.sum(share(weights, "row", ROWS), axis=0), "col", COLS)
    core, image_top = weights[:, :nb], weights[:, nb:]

    factor = jnp.linalg.cholesky(gram)
    solve = right_solve(factor, jnp.eye(nb, dtype=jnp.float32))
    g_inverse = newton_inverse_of_shifted(product(top_block, solve)).T
    image_top = product(image_top, solve)
    middle = product(product(solve.T, core), solve) + image_top + image_top.T + corner
    m_core = product(g_inverse.T, product(middle, g_inverse))
    solve_g = product(solve, g_inverse)

    def reflectors(panel, image, second, owner):
        size = panel.shape[0]
        picker = jnp.logical_and(
            lax.iota(jnp.int32, size)[:, None] - nb == lax.iota(jnp.int32, nb)[None, :], owner
        ).astype(jnp.float32)
        y_part = product3(panel, solve) + picker
        x_part = product3(image, solve_g) + product3(second, g_inverse)
        return y_part, x_part - 0.5 * product3(y_part, m_core)

    y_rows, z_rows = reflectors(panel_rows, image_rows, second_rows, row == 0)
    y_cols, z_cols = reflectors(panel_cols, image_cols, second_cols, col == 0)
    trail_out = updated - product3(
        jnp.concatenate([z_rows, y_rows], 1), jnp.concatenate([y_cols, z_cols], 1).T
    )
    return (trail_out, panel_out)


def solution(mesh):
    return jax.shard_map(
        shards,
        mesh=mesh,
        in_specs=(P("row", "col"), P(("row", "col"), None), P(("row", "col"), None), P(), P()),
        out_specs=(P("row", "col"), P(("row", "col"), None)),
        check_vma=False,
    )
```
